32 devices in a mesh: row: 2 (over x), col: 4 (over y, core), grid: 4 (over z).
Axes of the slice: x: 2, y: 2, z: 4, core: 2. Of those that a mesh axis runs over, the one named last changes fastest.
Arguments:
- snapshots: bfloat16 [16384, 1024], P(('row', 'col', 'grid')), may hold values from -6 to 6
- jitter_code: int32 [16384], replicated, may hold values from 0 to 63
- slab_start: int32 [4], P('grid'), may hold values from 0 to 127
- gamma: float32 [2048], P('grid'), may hold values from 0.1 to 10
- noise_var: float32 [1], replicated, may hold values from 0.3 to 1.5
Outputs:
- steered: float32 [16384, 2048], P(('row', 'col'), 'grid')
- gamma_new: float32 [2048], P('grid')
The draws below stay inside these ranges and needn't reach their ends.
All inputs are finite; a program needn't handle non-finite values.
Results may differ from the reference program's by a relative error of at most 0.0003.
Values may be sent and summed in bfloat16 or wider, within the bound.
A program may use at most 64 MiB of HBM per device.

```python
import math
import jax
import jax.numpy as jnp
from jax import lax

M = 16384
SNAP = 1024
SLAB = 512
GRID = 65536
POINTS = 2048
N_GRID = 4


def set_ends(drawn, rng, least, largest):
    longest = drawn.shape.index(max(drawn.shape))
    spots = []
    for shift in (0, 1):
        where = [jax.random.randint(jax.random.fold_in(rng, axis), (), 0, length) for axis, length in enumerate(drawn.shape)]
        where[longest] = (where[longest] + shift) % drawn.shape[longest]
        spots.append(tuple(where))
    return drawn.at[spots[0]].set(least).at[spots[1]].set(largest)


def level_of(stream_key, dims, shards, least, top_value):
    factor_of, own = 1.0, jax.random.fold_in(stream_key, 6)
    for dim, shards_of in shards:
        heights = jnp.exp(jax.random.uniform(jax.random.fold_in(own, dim), (shards_of,), jnp.float32, least / len(shards), top_value / len(shards)))
        factor_of = factor_of * jnp.repeat(heights, dims[dim] // shards_of).reshape([-1 if axis == dim else 1 for axis in range(len(dims))])
    return factor_of


def bell_draw(key, shape, width, most, cuts=(), kind=jnp.bfloat16):
    gain = level_of(key, shape, cuts, -0.22, 0.18) if cuts else 1.0
    array = jax.random.normal(key, shape, jnp.float32) * width * gain
    return jnp.minimum(jnp.maximum(array, -most), most).astype(kind)


def setup_inputs(seed: int = 0) -> dict:
    keys = jax.random.split(jax.random.key(seed), 6)
    snapshots = bell_draw(keys[0], (M, SNAP), 1.0, 6.0, ((0, 32),))
    jitter_code = set_ends(jax.random.randint(keys[1], (M,), 0, 64), jax.random.fold_in(keys[1], 1), 0, 63).astype(jnp.int32)
    slab_start = set_ends(jax.random.randint(keys[2], (N_GRID,), 0, GRID // SLAB), jax.random.fold_in(keys[2], 1), 0, (GRID // SLAB) - 1).astype(jnp.int32)
    gamma = jnp.clip(jnp.exp(math.log(10.0) - 4.6051702 * jax.random.uniform(keys[3], (POINTS,), jnp.float32) ** level_of(keys[3], (POINTS,), ((0, 4),), -0.2, 0.2)), 0.1, 10.0)
    noise_var = jnp.clip(jax.random.uniform(keys[4], (1,), jnp.float32, 0.3, 1.5), 0.3, 1.5)
    return dict(snapshots=snapshots, jitter_code=jitter_code, slab_start=slab_start, gamma=gamma, noise_var=noise_var)


def steer(sensor, codes, points):
    pos = (64 * sensor + codes + 32).astype(jnp.int32)[:, None]
    low = (points % 256).astype(jnp.int32)[None, :]
    high = (points // 256).astype(jnp.int32)[None, :]
    modulus = 64 * GRID
    first = (pos * low) % modulus
    second = ((pos * high) % (modulus // 256)) * 256
    wound = (first + second) % modulus
    turns = wound.astype(jnp.float32) / modulus - (pos % 128).astype(jnp.float32) / 128.0
    return jnp.cos(2.0 * jnp.pi * turns)


def reference(snapshots, jitter_code, slab_start, gamma, noise_var):
    sensors = jnp.arange(M, dtype=jnp.int32)
    stride = GRID // SLAB
    points = (slab_start[:, None] + stride * jnp.arange(SLAB, dtype=jnp.int32)[None, :]).reshape(-1).astype(jnp.int32)
    steering = steer(sensors, jitter_code, points)
    data = snapshots.astype(jnp.float32)
    projected = jnp.dot(data.T, steering, precision=lax.Precision.HIGHEST)
    steered = jnp.dot(data, projected, precision=lax.Precision.HIGHEST) / SNAP
    forms = jnp.sum(steering * steered, axis=0)
    norms = jnp.sum(steering * steering, axis=0)
    gamma_new = gamma * forms / (norms * (gamma + noise_var[0]))
    return steered, gamma_new
```

```python
import jax
import jax.numpy as jnp
from jax import lax
from jax.sharding import PartitionSpec as P

SNAP = 1024
GRID = 65536


def sine(turns):
    z = turns * turns
    p = jnp.float32(39.53581371)
    p = p * z + jnp.float32(-76.54965682)
    p = p * z + jnp.float32(81.60099819)
    p = p * z + jnp.float32(-41.34165493)
    p = p * z + jnp.float32(6.28318516)
    return p * turns


def steer(sensor, codes, points):
    pos = 64 * sensor + codes + 32
    phase = (pos[:, None] * points[None, :] - ((pos & 127) << 15)[:, None]) << 10
    turns = phase.astype(jnp.float32) * jnp.float32(2.0**-32)
    return sine(0.25 - jnp.abs(turns))


def split(x):
    hi = lax.reduce_precision(x, 8, 7)
    lo = x - hi
    return hi.astype(jnp.bfloat16), lo.astype(jnp.bfloat16)


def on_device(snapshots, jitter_code, slab_start, gamma, noise_var):
    n_col = lax.axis_size("col")
    n_grid = lax.axis_size("grid")
    own_count = snapshots.shape[0]
    group_rows = own_count * n_grid
    block_rows = group_rows * n_col
    row_id = lax.axis_index("row")
    col_id = lax.axis_index("col")
    slab_len = gamma.shape[0]
    stride = GRID // slab_len
    points = slab_start[0] + stride * jnp.arange(slab_len, dtype=jnp.int32)
    base = row_id * block_rows + col_id * group_rows
    own_sensors = base + jnp.arange(group_rows, dtype=jnp.int32)
    codes = lax.dynamic_slice(jitter_code, (base,), (group_rows,))
    own_snaps = lax.all_gather(snapshots, "grid", axis=0, tiled=True)
    own_steer = steer(own_sensors, codes, points)
    hi, lo = split(own_steer)
    dn = (((0,), (0,)), ((), ()))
    f32 = jnp.float32
    partial_value = lax.dot_general(own_snaps, hi, dn, preferred_element_type=f32)
    partial_value += lax.dot_general(own_snaps, lo, dn, preferred_element_type=f32)
    projected, norms = lax.psum(
        (partial_value, jnp.sum(own_steer * own_steer, axis=0)), ("row", "col")
    )
    hi, lo = split(projected)
    steered = jnp.dot(own_snaps, hi, preferred_element_type=f32)
    steered += jnp.dot(own_snaps, lo, preferred_element_type=f32)
    steered = steered / SNAP
    forms = jnp.sum(projected * projected, axis=0) / SNAP
    gamma_new = gamma * forms / (norms * (gamma + noise_var[0]))
    return (steered, gamma_new)


def solution(mesh):
    in_specs = (P(("row", "col", "grid"), None), P(), P("grid"), P("grid"), P())
    out_specs = (P(("row", "col"), "grid"), P("grid"))
    return jax.shard_map(
        on_device, mesh=mesh, in_specs=in_specs, out_specs=out_specs, check_vma=False
    )
```

```python
import functools

import jax
import jax.numpy as jnp
from jax import lax
from jax.experimental import pallas as pl
from jax.experimental.pallas import tpu as pltpu
from jax.sharding import PartitionSpec as P

GRID = 65536
WIDTH = 256
F32 = jnp.float32
BF16 = jnp.bfloat16
MESH = pl.DeviceIdType.MESH


def sine(turns):
    z = turns * turns
    p = F32(39.53581371)
    p = p * z + F32(-76.54965682)
    p = p * z + F32(81.60099819)
    p = p * z + F32(-41.34165493)
    p = p * z + F32(6.28318516)
    return p * turns


def split(x):
    hi = x.astype(BF16)
    return hi, (x - hi.astype(F32)).astype(BF16)


def kernel(
    sizes, start_ref, pos_ref, snaps_ref, out_ref, forms_ref, norms_ref,
    held, steer_hi, steer_lo, part, part_norm, full, proj_hi, proj_lo, *rest,
):
    n_row, n_col, n_grid, stride = sizes
    dims = [d for d in ((2, "core"), (n_col // 2, "y"), (n_row, "row")) if d[0] > 1]
    landed, sums = rest[: len(dims)], rest[len(dims) : 2 * len(dims)]
    load_sem, z_send, z_recv, p_send, p_recv = rest[2 * len(dims) :]
    n_block, _, rows, width = held.shape
    points = part.shape[0]
    snap = n_block * width
    row, col, z = (lax.axis_index(a) for a in ("row", "col", "grid"))
    place = {"core": col % 2, "y": col // 2, "row": row}

    def peer(kind, n, p):
        other = lax.rem(place[kind] + p, n)
        if kind == "row":
            return (other, col, z)
        if kind == "core":
            return (row, (col // 2) * 2 + other, z)
        return (row, other * 2 + col % 2, z)

    peers = [peer(kind, n, p) for n, kind in dims for p in range(1, n)]
    up, down = (row, col, z + 1), (row, col, z - 1)
    loads = [
        pltpu.make_async_copy(
            snaps_ref.at[:, pl.ds(k * width, width)], held.at[k, z], load_sem.at[k]
        )
        for k in range(n_block)
    ]
    for load in loads:
        load.start()
    barrier = pltpu.get_barrier_semaphore()
    for device in peers:
        pl.semaphore_signal(barrier, inc=1, device_id=device, device_id_type=MESH)

    @pl.when(z + 1 < n_grid)
    def _():
        pl.semaphore_signal(barrier, inc=1, device_id=up, device_id_type=MESH)

    @pl.when(z > 0)
    def _():
        pl.semaphore_signal(barrier, inc=1, device_id=down, device_id_type=MESH)

    beside = jnp.minimum(z, 1) + jnp.minimum(n_grid - 1 - z, 1)
    pl.semaphore_wait(barrier, len(peers) + beside)

    def hop(k, s, direction, origin):
        return pltpu.make_async_remote_copy(
            src_ref=held.at[k, origin],
            dst_ref=held.at[k, origin],
            send_sem=z_send.at[direction, k, s],
            recv_sem=z_recv.at[direction, k, s],
            device_id=up if direction == 0 else down,
            device_id_type=MESH,
        )

    def can_send(s, direction):
        if direction == 0:
            return jnp.logical_and(z + 1 < n_grid, z - s >= 0), z - s
        return jnp.logical_and(z > 0, z + s < n_grid), z + s

    def can_receive(s, direction):
        if direction == 0:
            return z - s - 1 >= 0, z - s - 1
        return z + s + 1 < n_grid, z + s + 1

    def send(k, s):
        for direction in (0, 1):
            ok, origin = can_send(s, direction)

            @pl.when(ok)
            def _():
                hop(k, s, direction, origin).start()

    def receive(k, s):
        for direction in (0, 1):
            ok, origin = can_receive(s, direction)

            @pl.when(ok)
            def _():
                hop(k, s, direction, origin).wait_recv()

    def drain(k, s):
        for direction in (0, 1):
            ok, origin = can_send(s, direction)

            @pl.when(ok)
            def _():
                hop(k, s, direction, origin).wait_send()

    def reduce_steps(source, target):
        lanes = pl.ds(0, source.shape[1])
        offsets, sems, at, count = [], [], 0, 0
        length = points
        for n, kind in dims:
            length //= n
            offsets.append((at, length))
            at = at + place[kind] * length
            sems.append(count)
            count += n - 1

        def aligned(index):
            return pl.multiple_of(index, 8)

        def scatter(a):
            n, kind = dims[a]
            size = offsets[a][1]
            cur = source if a == 0 else sums[a - 1].at[:, lanes]
            copies = []
            for p in range(1, n):
                other = lax.rem(place[kind] + p, n)
                copy = pltpu.make_async_remote_copy(
                    src_ref=cur.at[pl.ds(aligned(other * size), size), :],
                    dst_ref=landed[a].at[p - 1, :, lanes],
                    send_sem=p_send.at[0, sems[a] + p - 1],
                    recv_sem=p_recv.at[0, sems[a] + p - 1],
                    device_id=peer(kind, n, p),
                    device_id_type=MESH,
                )
                copy.start()
                copies.append(copy)
            for copy in copies:
                copy.wait()
            total = cur[pl.ds(aligned(place[kind] * size), size), :]
            for p in range(1, n):
                total = total + landed[a][p - 1, :, lanes]
            if a + 1 < len(dims):
                sums[a][:, lanes] = total
            else:
                target[pl.ds(aligned(at), size), :] = total

        def gather(a):
            n, kind = dims[a]
            base, size = offsets[a]
            mine = pl.ds(aligned(base + place[kind] * size), size)
            copies = []
            for p in range(1, n):
                copy = pltpu.make_async_remote_copy(
                    src_ref=target.at[mine, :],
                    dst_ref=target.at[mine, :],
                    send_sem=p_send.at[1, sems[a] + p - 1],
                    recv_sem=p_recv.at[1, sems[a] + p - 1],
                    device_id=peer(kind, n, p),
                    device_id_type=MESH,
                )
                copy.start()
                copies.append(copy)
            for copy in copies:
                copy.wait()

        steps = [functools.partial(scatter, a) for a in range(len(dims))]
        return steps + [functools.partial(gather, a) for a in reversed(range(len(dims)))]

    def steer():
        part_norm[...] = jnp.zeros_like(part_norm)
        tile = 16
        tiles = points // tile

        def body(i, carry):
            g, first = i // tiles, pl.multiple_of((i % tiles) * tile, tile)
            pos = pos_ref[g]
            point = start_ref[0] + stride * (
                first + lax.broadcasted_iota(jnp.int32, (tile, 1), 0)
            )
            phase = (point * pos - ((pos & 127) << 15)) << 10
            turns = phase.astype(F32) * F32(2.0**-32)
            value = sine(0.25 - jnp.abs(turns))
            hi, lo = split(value)
            steer_hi[g, pl.ds(first, tile), :] = hi
            steer_lo[g, pl.ds(first, tile), :] = lo
            square = jnp.sum(value * value, axis=1, keepdims=True)
            part_norm[pl.ds(first, tile), :] += jnp.broadcast_to(square, (tile, 128))
            return carry

        lax.fori_loop(0, n_grid * tiles, body, 0)

    def project(k):
        part[...] = jnp.zeros_like(part)

        def body(g, carry):
            block = held[k, g]
            part[...] += jnp.dot(steer_hi[g], block, preferred_element_type=F32) + jnp.dot(
                steer_lo[g], block, preferred_element_type=F32
            )
            return carry

        lax.fori_loop(0, n_grid, body, 0)

    def apply(k):
        value = full[k]
        square = jnp.sum(value * value, axis=1, keepdims=True)
        square = jnp.broadcast_to(square, (points, 128))
        forms_ref[...] = square if k == 0 else forms_ref[...] + square
        hi, lo = split(value / snap)
        proj_hi[...] = hi
        proj_lo[...] = lo
        dims_nt = (((1,), (1,)), ((), ()))

        def body(g, carry):
            block = held[k, g]
            added = lax.dot_general(block, proj_hi[...], dims_nt, preferred_element_type=F32)
            added += lax.dot_general(block, proj_lo[...], dims_nt, preferred_element_type=F32)
            spot = pl.ds(pl.multiple_of(g * rows, rows), rows)
            out_ref[spot, :] = added if k == 0 else out_ref[spot, :] + added
            return carry

        lax.fori_loop(0, n_grid, body, 0)

    loads[0].wait()
    send(0, 0)
    for load in loads[1:]:
        load.wait()
    steer()
    last = n_grid - 2
    queue = reduce_steps(part_norm, norms_ref)
    for k in range(n_block):
        for s in range(n_grid - 1):
            if k > 0 and s == 0:
                project(k - 1)
                queue = reduce_steps(part, full.at[k - 1])
            share = -(-len(queue) // (n_grid - 1 - s))
            todo, queue = queue[:share], queue[share:]
            for step in todo[:1]:
                step()
            receive(k, s)
            if s < last:
                send(k, s + 1)
            if s + 1 == last and k + 1 < n_block:
                send(k + 1, 0)
            for step in todo[1:]:
                step()
            if k > 1 and s == 0:
                apply(k - 2)
    project(n_block - 1)
    if n_block > 1:
        apply(n_block - 2)
    for step in reduce_steps(part, full.at[n_block - 1]):
        step()
    apply(n_block - 1)
    for k in range(n_block):
        for s in range(n_grid - 1):
            drain(k, s)


def on_device(snapshots, jitter_code, slab_start, gamma, noise_var):
    n_row, n_col, n_grid = (lax.axis_size(a) for a in ("row", "col", "grid"))
    rows, snap = snapshots.shape
    group_rows = rows * n_grid
    points = gamma.shape[0]
    base = (lax.axis_index("row") * n_col + lax.axis_index("col")) * group_rows
    sensors = base + jnp.arange(group_rows, dtype=jnp.int32)
    pos = 64 * sensors + lax.dynamic_slice(jitter_code, (base,), (group_rows,)) + 32
    width = min(WIDTH, snap)
    n_block = snap // width
    dims = [n for n in (2, n_col // 2, n_row) if n > 1]
    landed, sums, length = [], [], points
    for n in dims:
        length //= n
        landed.append(pltpu.VMEM((n - 1, length, width), F32))
        sums.append(pltpu.VMEM((length, width), F32))
    n_peers = sum(n - 1 for n in dims)
    vmem = pl.BlockSpec(memory_space=pltpu.VMEM)
    steered, forms, norms = pl.pallas_call(
        functools.partial(kernel, (n_row, n_col, n_grid, GRID // points)),
        out_shape=(
            jax.ShapeDtypeStruct((group_rows, points), F32),
            jax.ShapeDtypeStruct((points, 128), F32),
            jax.ShapeDtypeStruct((points, 128), F32),
        ),
        in_specs=[
            pl.BlockSpec(memory_space=pltpu.SMEM),
            vmem,
            pl.BlockSpec(memory_space=pl.ANY),
        ],
        out_specs=(vmem, vmem, vmem),
        scratch_shapes=[
            pltpu.VMEM((n_block, n_grid, rows, width), BF16),
            pltpu.VMEM((n_grid, points, rows), BF16),
            pltpu.VMEM((n_grid, points, rows), BF16),
            pltpu.VMEM((points, width), F32),
            pltpu.VMEM((points, 128), F32),
            pltpu.VMEM((n_block, points, width), F32),
            pltpu.VMEM((points, width), BF16),
            pltpu.VMEM((points, width), BF16),
            *landed,
            *sums,
            pltpu.SemaphoreType.DMA((n_block,)),
            pltpu.SemaphoreType.DMA((2, n_block, n_grid - 1)),
            pltpu.SemaphoreType.DMA((2, n_block, n_grid - 1)),
            pltpu.SemaphoreType.DMA((2, n_peers)),
            pltpu.SemaphoreType.DMA((2, n_peers)),
        ],
        compiler_params=pltpu.CompilerParams(
            collective_id=0, has_side_effects=True, vmem_limit_bytes=56 << 20
        ),
    )(slab_start, pos.reshape(n_grid, 1, rows), snapshots)
    forms = forms[:, 0] / snap
    gamma_new = gamma * forms / (norms[:, 0] * (gamma + noise_var[0]))
    return (steered, gamma_new)


def solution(mesh):
    in_specs = (P(("row", "col", "grid"), None), P(), P("grid"), P("grid"), P())
    out_specs = (P(("row", "col"), "grid"), P("grid"))
    return jax.shard_map(
        on_device, mesh=mesh, in_specs=in_specs, out_specs=out_specs, check_vma=False
    )
```

```python
import functools

import jax
import jax.numpy as jnp
from jax import lax
from jax.experimental import pallas as pl
from jax.experimental.pallas import tpu as pltpu
from jax.sharding import PartitionSpec as P

GRID = 65536
WIDTH = 256
F32 = jnp.float32
BF16 = jnp.bfloat16
MESH = pl.DeviceIdType.MESH


def sine(turns):
    z = turns * turns
    p = F32(39.53581371)
    p = p * z + F32(-76.54965682)
    p = p * z + F32(81.60099819)
    p = p * z + F32(-41.34165493)
    p = p * z + F32(6.28318516)
    return p * turns


def split(x):
    hi = x.astype(BF16)
    return hi, (x - hi.astype(F32)).astype(BF16)


def kernel(
    sizes, start_ref, pos_ref, snaps_ref, out_ref, forms_ref, norms_ref,
    held, steer_hi, steer_lo, part, part_norm, full, proj_hi, proj_lo, *rest,
):
    n_row, n_col, n_grid, stride = sizes
    dims = [d for d in ((2, "core"), (n_col // 2, "y"), (n_row, "row")) if d[0] > 1]
    landed, sums = rest[: len(dims)], rest[len(dims) : 2 * len(dims)]
    load_sem, z_send, z_recv, p_send, p_recv = rest[2 * len(dims) :]
    n_block, _, rows, width = held.shape
    points = part.shape[1]
    snap = n_block * width
    row, col, z = (lax.axis_index(a) for a in ("row", "col", "grid"))
    place = {"core": col % 2, "y": col // 2, "row": row}

    def peer(kind, n, p):
        other = lax.rem(place[kind] + p, n)
        if kind == "row":
            return (other, col, z)
        if kind == "core":
            return (row, (col // 2) * 2 + other, z)
        return (row, other * 2 + col % 2, z)

    peers = [peer(kind, n, p) for n, kind in dims for p in range(1, n)]
    up, down = (row, col, z + 1), (row, col, z - 1)
    loads = [
        pltpu.make_async_copy(
            snaps_ref.at[:, pl.ds(k * width, width)], held.at[k, z], load_sem.at[k]
        )
        for k in range(n_block)
    ]
    for load in loads:
        load.start()
    barrier = pltpu.get_barrier_semaphore()
    for device in peers:
        pl.semaphore_signal(barrier, inc=1, device_id=device, device_id_type=MESH)

    @pl.when(z + 1 < n_grid)
    def _():
        pl.semaphore_signal(barrier, inc=1, device_id=up, device_id_type=MESH)

    @pl.when(z > 0)
    def _():
        pl.semaphore_signal(barrier, inc=1, device_id=down, device_id_type=MESH)

    beside = jnp.minimum(z, 1) + jnp.minimum(n_grid - 1 - z, 1)
    pl.semaphore_wait(barrier, len(peers) + beside)

    def hop(k, s, direction, origin):
        return pltpu.make_async_remote_copy(
            src_ref=held.at[k, origin],
            dst_ref=held.at[k, origin],
            send_sem=z_send.at[direction, k, s],
            recv_sem=z_recv.at[direction, k, s],
            device_id=up if direction == 0 else down,
            device_id_type=MESH,
        )

    def can_send(s, direction):
        if direction == 0:
            return jnp.logical_and(z + 1 < n_grid, z - s >= 0), z - s
        return jnp.logical_and(z > 0, z + s < n_grid), z + s

    def can_receive(s, direction):
        if direction == 0:
            return z - s - 1 >= 0, z - s - 1
        return z + s + 1 < n_grid, z + s + 1

    def send(k, s):
        for direction in (0, 1):
            ok, origin = can_send(s, direction)

            @pl.when(ok)
            def _():
                hop(k, s, direction, origin).start()

    def receive(k, s):
        for direction in (0, 1):
            ok, origin = can_receive(s, direction)

            @pl.when(ok)
            def _():
                hop(k, s, direction, origin).wait_recv()

    def drain(k, s):
        for direction in (0, 1):
            ok, origin = can_send(s, direction)

            @pl.when(ok)
            def _():
                hop(k, s, direction, origin).wait_send()

    def reduce_steps(source, target):
        lanes = pl.ds(0, source.shape[1])
        offsets, sems, at, count = [], [], 0, 0
        length = points
        for n, kind in dims:
            length //= n
            offsets.append((at, length))
            at = at + place[kind] * length
            sems.append(count)
            count += n - 1

        def aligned(index):
            return pl.multiple_of(index, 8)

        def scatter(a):
            n, kind = dims[a]
            size = offsets[a][1]
            cur = source if a == 0 else sums[a - 1].at[:, lanes]
            copies = []
            yield
            for p in range(1, n):
                other = lax.rem(place[kind] + p, n)
                copy = pltpu.make_async_remote_copy(
                    src_ref=cur.at[pl.ds(aligned(other * size), size), :],
                    dst_ref=landed[a].at[p - 1, :, lanes],
                    send_sem=p_send.at[0, sems[a] + p - 1],
                    recv_sem=p_recv.at[0, sems[a] + p - 1],
                    device_id=peer(kind, n, p),
                    device_id_type=MESH,
                )
                copy.start()
                copies.append(copy)
            yield
            for copy in copies:
                copy.wait()
            total = cur[pl.ds(aligned(place[kind] * size), size), :]
            for p in range(1, n):
                total = total + landed[a][p - 1, :, lanes]
            if a + 1 < len(dims):
                sums[a][:, lanes] = total
            else:
                target[pl.ds(aligned(at), size), :] = total
            yield

        def gather(a):
            n, kind = dims[a]
            base, size = offsets[a]
            mine = pl.ds(aligned(base + place[kind] * size), size)
            copies = []
            yield
            for p in range(1, n):
                copy = pltpu.make_async_remote_copy(
                    src_ref=target.at[mine, :],
                    dst_ref=target.at[mine, :],
                    send_sem=p_send.at[1, sems[a] + p - 1],
                    recv_sem=p_recv.at[1, sems[a] + p - 1],
                    device_id=peer(kind, n, p),
                    device_id_type=MESH,
                )
                copy.start()
                copies.append(copy)
            yield
            for copy in copies:
                copy.wait()
            yield

        steps = [scatter(a) for a in range(len(dims))]
        steps += [gather(a) for a in reversed(range(len(dims)))]
        for step in steps:
            next(step)
        return steps

    def steer():
        part_norm[...] = jnp.zeros_like(part_norm)
        tile = 16
        tiles = points // tile

        def body(i, carry):
            g, first = i // tiles, pl.multiple_of((i % tiles) * tile, tile)
            pos = pos_ref[g]
            point = start_ref[0] + stride * (
                first + lax.broadcasted_iota(jnp.int32, (tile, 1), 0)
            )
            phase = (point * pos - ((pos & 127) << 15)) << 10
            turns = phase.astype(F32) * F32(2.0**-32)
            value = sine(0.25 - jnp.abs(turns))
            hi, lo = split(value)
            steer_hi[g, pl.ds(first, tile), :] = hi
            steer_lo[g, pl.ds(first, tile), :] = lo
            square = jnp.sum(value * value, axis=1, keepdims=True)
            part_norm[pl.ds(first, tile), :] += jnp.broadcast_to(square, (tile, 128))
            return carry

        lax.fori_loop(0, n_grid * tiles, body, 0)

    def project(k, origin, fresh=False):
        block = held[k, origin]
        value = jnp.dot(steer_hi[origin], block, preferred_element_type=F32)
        value += jnp.dot(steer_lo[origin], block, preferred_element_type=F32)
        if fresh:
            part[k % 2] = value
        else:
            part[k % 2] += value

    def project_arrived(k, s):
        for direction in (0, 1):
            ok, origin = can_receive(s, direction)

            @pl.when(ok)
            def _():
                project(k, origin)

    def prepare(k):
        value = full[k]
        square = jnp.sum(value * value, axis=1, keepdims=True)
        square = jnp.broadcast_to(square, (points, 128))
        forms_ref[...] = square if k == 0 else forms_ref[...] + square
        hi, lo = split(value / snap)
        proj_hi[...] = hi
        proj_lo[...] = lo

    def apply(k, first, count):
        dims_nt = (((1,), (1,)), ((), ()))

        def body(g, carry):
            block = held[k, g]
            added = lax.dot_general(block, proj_hi[...], dims_nt, preferred_element_type=F32)
            added += lax.dot_general(block, proj_lo[...], dims_nt, preferred_element_type=F32)
            spot = pl.ds(pl.multiple_of(g * rows, rows), rows)
            out_ref[spot, :] = added if k == 0 else out_ref[spot, :] + added
            return carry

        lax.fori_loop(first, first + count, body, 0)

    def applied(k, s, rounds):
        if k < 0:
            return
        if s == 0:
            prepare(k)
        first, end = n_grid * s // rounds, n_grid * (s + 1) // rounds
        if end > first:
            apply(k, first, end - first)

    loads[0].wait()
    send(0, 0)
    if n_block > 1:
        loads[1].wait()
        send(1, 0)
    for load in loads[2:]:
        load.wait()
    steer()
    rounds = n_grid - 1
    queue = reduce_steps(part_norm, norms_ref)
    for k in range(n_block):
        for s in range(rounds):
            share = -(-len(queue) // (rounds - s))
            todo, queue = queue[:share], queue[share:]
            for step in todo[:1]:
                next(step)
            if s == 0:
                project(k, z, fresh=True)
            receive(k, s)
            if s + 1 < rounds:
                send(k, s + 1)
            if s + 2 == rounds and k + 2 < n_block:
                send(k + 2, 0)
            for step in todo[:1]:
                next(step)
            for step in todo[1:2]:
                next(step)
            project_arrived(k, s)
            applied(k - 2, s, rounds)
            for step in todo[1:2]:
                next(step)
            for step in todo[2:]:
                next(step)
                next(step)
        queue = reduce_steps(part.at[k % 2], full.at[k])
    for i, step in enumerate(queue):
        next(step)
        applied(n_block - 2, i, len(queue))
        next(step)
    applied(n_block - 1, 0, 1)
    for k in range(n_block):
        for s in range(n_grid - 1):
            drain(k, s)


def on_device(snapshots, jitter_code, slab_start, gamma, noise_var):
    n_row, n_col, n_grid = (lax.axis_size(a) for a in ("row", "col", "grid"))
    rows, snap = snapshots.shape
    group_rows = rows * n_grid
    points = gamma.shape[0]
    base = (lax.axis_index("row") * n_col + lax.axis_index("col")) * group_rows
    sensors = base + jnp.arange(group_rows, dtype=jnp.int32)
    pos = 64 * sensors + lax.dynamic_slice(jitter_code, (base,), (group_rows,)) + 32
    width = min(WIDTH, snap)
    n_block = snap // width
    dims = [n for n in (2, n_col // 2, n_row) if n > 1]
    landed, sums, length = [], [], points
    for n in dims:
        length //= n
        landed.append(pltpu.VMEM((n - 1, length, width), F32))
        sums.append(pltpu.VMEM((length, width), F32))
    n_peers = sum(n - 1 for n in dims)
    vmem = pl.BlockSpec(memory_space=pltpu.VMEM)
    steered, forms, norms = pl.pallas_call(
        functools.partial(kernel, (n_row, n_col, n_grid, GRID // points)),
        out_shape=(
            jax.ShapeDtypeStruct((group_rows, points), F32),
            jax.ShapeDtypeStruct((points, 128), F32),
            jax.ShapeDtypeStruct((points, 128), F32),
        ),
        in_specs=[
            pl.BlockSpec(memory_space=pltpu.SMEM),
            vmem,
            pl.BlockSpec(memory_space=pl.ANY),
        ],
        out_specs=(vmem, vmem, vmem),
        scratch_shapes=[
            pltpu.VMEM((n_block, n_grid, rows, width), BF16),
            pltpu.VMEM((n_grid, points, rows), BF16),
            pltpu.VMEM((n_grid, points, rows), BF16),
            pltpu.VMEM((2, points, width), F32),
            pltpu.VMEM((points, 128), F32),
            pltpu.VMEM((n_block, points, width), F32),
            pltpu.VMEM((points, width), BF16),
            pltpu.VMEM((points, width), BF16),
            *landed,
            *sums,
            pltpu.SemaphoreType.DMA((n_block,)),
            pltpu.SemaphoreType.DMA((2, n_block, n_grid - 1)),
            pltpu.SemaphoreType.DMA((2, n_block, n_grid - 1)),
            pltpu.SemaphoreType.DMA((2, n_peers)),
            pltpu.SemaphoreType.DMA((2, n_peers)),
        ],
        compiler_params=pltpu.CompilerParams(
            collective_id=0, has_side_effects=True, vmem_limit_bytes=56 << 20
        ),
    )(slab_start, pos.reshape(n_grid, 1, rows), snapshots)
    forms = forms[:, 0] / snap
    gamma_new = gamma * forms / (norms[:, 0] * (gamma + noise_var[0]))
    return (steered, gamma_new)


def solution(mesh):
    in_specs = (P(("row", "col", "grid"), None), P(), P("grid"), P("grid"), P())
    out_specs = (P(("row", "col"), "grid"), P("grid"))
    return jax.shard_map(
        on_device, mesh=mesh, in_specs=in_specs, out_specs=out_specs, check_vma=False
    )
```

```python
import functools

import jax
import jax.numpy as jnp
from jax import lax
from jax.experimental import pallas as pl
from jax.experimental.pallas import tpu as pltpu
from jax.sharding import PartitionSpec as P

GRID = 65536
WIDTH = 256
F32 = jnp.float32
BF16 = jnp.bfloat16
MESH = pl.DeviceIdType.MESH


def sine(turns):
    z = turns * turns
    p = F32(39.53581371)
    p = p * z + F32(-76.54965682)
    p = p * z + F32(81.60099819)
    p = p * z + F32(-41.34165493)
    p = p * z + F32(6.28318516)
    return p * turns


def split(x):
    hi = x.astype(BF16)
    return hi, (x - hi.astype(F32)).astype(BF16)


def kernel(
    sizes, start_ref, pos_ref, snaps_ref, out_ref, forms_ref, norms_ref,
    held, steer_hi, steer_lo, part, part_norm, full, proj_hi, proj_lo, *rest,
):
    n_row, n_col, n_grid, stride = sizes
    dims = [d for d in ((2, "core"), (n_col // 2, "y"), (n_row, "row")) if d[0] > 1]
    landed, sums = rest[: len(dims)], rest[len(dims) : 2 * len(dims)]
    load_sem, z_send, z_recv, p_send, p_recv = rest[2 * len(dims) :]
    n_block, _, rows, width = held.shape
    points = part.shape[1]
    snap = n_block * width
    row, col, z = (lax.axis_index(a) for a in ("row", "col", "grid"))
    place = {"core": col % 2, "y": col // 2, "row": row}

    def peer(kind, n, p):
        other = lax.rem(place[kind] + p, n)
        if kind == "row":
            return (other, col, z)
        if kind == "core":
            return (row, (col // 2) * 2 + other, z)
        return (row, other * 2 + col % 2, z)

    peers = [peer(kind, n, p) for n, kind in dims for p in range(1, n)]
    up, down = (row, col, z + 1), (row, col, z - 1)
    loads = [
        pltpu.make_async_copy(
            snaps_ref.at[:, pl.ds(k * width, width)], held.at[k, z], load_sem.at[k]
        )
        for k in range(n_block)
    ]
    for load in loads:
        load.start()
    barrier = pltpu.get_barrier_semaphore()
    for device in peers:
        pl.semaphore_signal(barrier, inc=1, device_id=device, device_id_type=MESH)

    @pl.when(z + 1 < n_grid)
    def _():
        pl.semaphore_signal(barrier, inc=1, device_id=up, device_id_type=MESH)

    @pl.when(z > 0)
    def _():
        pl.semaphore_signal(barrier, inc=1, device_id=down, device_id_type=MESH)

    beside = jnp.minimum(z, 1) + jnp.minimum(n_grid - 1 - z, 1)
    pl.semaphore_wait(barrier, len(peers) + beside)

    def hop(k, s, direction, origin):
        return pltpu.make_async_remote_copy(
            src_ref=held.at[k, origin],
            dst_ref=held.at[k, origin],
            send_sem=z_send.at[direction, k, s],
            recv_sem=z_recv.at[direction, k, s],
            device_id=up if direction == 0 else down,
            device_id_type=MESH,
        )

    def can_send(s, direction):
        if direction == 0:
            return jnp.logical_and(z + 1 < n_grid, z - s >= 0), z - s
        return jnp.logical_and(z > 0, z + s < n_grid), z + s

    def can_receive(s, direction):
        if direction == 0:
            return z - s - 1 >= 0, z - s - 1
        return z + s + 1 < n_grid, z + s + 1

    def send(k, s):
        for direction in (0, 1):
            ok, origin = can_send(s, direction)

            @pl.when(ok)
            def _():
                hop(k, s, direction, origin).start()

    def receive(k, s):
        for direction in (0, 1):
            ok, origin = can_receive(s, direction)

            @pl.when(ok)
            def _():
                hop(k, s, direction, origin).wait_recv()

    def drain(k, s):
        for direction in (0, 1):
            ok, origin = can_send(s, direction)

            @pl.when(ok)
            def _():
                hop(k, s, direction, origin).wait_send()

    def reduce_steps(source, target, turn):
        lanes = pl.ds(0, source.shape[1])
        offsets, sems, at, count = [], [], 0, 0
        length = points
        for n, kind in dims:
            length //= n
            offsets.append((at, length))
            at = at + place[kind] * length
            sems.append(count)
            count += n - 1

        def aligned(index):
            return pl.multiple_of(index, 8)

        def scatter(a):
            n, kind = dims[a]
            size = offsets[a][1]
            cur = source if a == 0 else sums[a - 1].at[:, lanes]
            copies = []
            yield
            for p in range(1, n):
                other = lax.rem(place[kind] + p, n)
                copy = pltpu.make_async_remote_copy(
                    src_ref=cur.at[pl.ds(aligned(other * size), size), :],
                    dst_ref=landed[a].at[turn, p - 1, :, lanes],
                    send_sem=p_send.at[2 * turn, sems[a] + p - 1],
                    recv_sem=p_recv.at[2 * turn, sems[a] + p - 1],
                    device_id=peer(kind, n, p),
                    device_id_type=MESH,
                )
                copy.start()
                copies.append(copy)
            yield
            for copy in copies:
                copy.wait()
            total = cur[pl.ds(aligned(place[kind] * size), size), :]
            for p in range(1, n):
                total = total + landed[a][turn, p - 1, :, lanes]
            if a + 1 < len(dims):
                sums[a][:, lanes] = total
            else:
                target[pl.ds(aligned(at), size), :] = total
            yield

        def gather(a):
            n, kind = dims[a]
            base, size = offsets[a]
            mine = pl.ds(aligned(base + place[kind] * size), size)
            copies = []
            yield
            for p in range(1, n):
                copy = pltpu.make_async_remote_copy(
                    src_ref=target.at[mine, :],
                    dst_ref=target.at[mine, :],
                    send_sem=p_send.at[2 * turn + 1, sems[a] + p - 1],
                    recv_sem=p_recv.at[2 * turn + 1, sems[a] + p - 1],
                    device_id=peer(kind, n, p),
                    device_id_type=MESH,
                )
                copy.start()
                copies.append(copy)
            yield
            for copy in copies:
                copy.wait()
            yield

        scatters = [scatter(a) for a in range(len(dims))]
        gathers = [gather(a) for a in reversed(range(len(dims)))]
        for step in scatters + gathers:
            next(step)
        return scatters, gathers

    def steer():
        part_norm[...] = jnp.zeros_like(part_norm)
        tile = 16
        tiles = points // tile

        def body(i, carry):
            g, first = i // tiles, pl.multiple_of((i % tiles) * tile, tile)
            pos = pos_ref[g]
            point = start_ref[0] + stride * (
                first + lax.broadcasted_iota(jnp.int32, (tile, 1), 0)
            )
            phase = (point * pos - ((pos & 127) << 15)) << 10
            turns = phase.astype(F32) * F32(2.0**-32)
            value = sine(0.25 - jnp.abs(turns))
            hi, lo = split(value)
            steer_hi[g, pl.ds(first, tile), :] = hi
            steer_lo[g, pl.ds(first, tile), :] = lo
            square = jnp.sum(value * value, axis=1, keepdims=True)
            part_norm[pl.ds(first, tile), :] += jnp.broadcast_to(square, (tile, 128))
            return carry

        lax.fori_loop(0, n_grid * tiles, body, 0)

    def project(k, origin, fresh=False):
        block = held[k, origin]
        value = jnp.dot(steer_hi[origin], block, preferred_element_type=F32)
        value += jnp.dot(steer_lo[origin], block, preferred_element_type=F32)
        if fresh:
            part[k % 2] = value
        else:
            part[k % 2] += value

    def project_arrived(k, s):
        for direction in (0, 1):
            ok, origin = can_receive(s, direction)

            @pl.when(ok)
            def _():
                project(k, origin)

    def prepare(k):
        value = full[k]
        square = jnp.sum(value * value, axis=1, keepdims=True)
        square = jnp.broadcast_to(square, (points, 128))
        forms_ref[...] = square if k == 0 else forms_ref[...] + square
        hi, lo = split(value / snap)
        proj_hi[...] = hi
        proj_lo[...] = lo

    def apply(k, first, count):
        dims_nt = (((1,), (1,)), ((), ()))

        def body(g, carry):
            block = held[k, g]
            added = lax.dot_general(block, proj_hi[...], dims_nt, preferred_element_type=F32)
            added += lax.dot_general(block, proj_lo[...], dims_nt, preferred_element_type=F32)
            spot = pl.ds(pl.multiple_of(g * rows, rows), rows)
            out_ref[spot, :] = added if k == 0 else out_ref[spot, :] + added
            return carry

        lax.fori_loop(first, first + count, body, 0)

    def applied(k, s, rounds):
        if k < 0:
            return
        if s == 0:
            prepare(k)
        first, end = n_grid * s // rounds, n_grid * (s + 1) // rounds
        if end > first:
            apply(k, first, end - first)

    loads[0].wait()
    send(0, 0)
    if n_block > 1:
        loads[1].wait()
        send(1, 0)
    for load in loads[2:]:
        load.wait()
    steer()
    rounds = n_grid - 1
    def advance(steps):
        for step in steps:
            next(step)

    def extra(*lists):
        for steps in lists:
            for step in steps[rounds:]:
                next(step)
                next(step)

    scatters, gathers = reduce_steps(part_norm, norms_ref, 1)
    waiting = []
    for k in range(n_block):
        for s in range(rounds):
            slot = scatters[s : s + 1] + waiting[s : s + 1]
            advance(slot)
            if s == 0:
                project(k, z, fresh=True)
            receive(k, s)
            if s + 1 < rounds:
                send(k, s + 1)
            if s + 2 == rounds and k + 2 < n_block:
                send(k + 2, 0)
            project_arrived(k, s)
            applied(k - 3, s, rounds)
            advance(slot)
        extra(scatters, waiting)
        waiting = gathers
        scatters, gathers = reduce_steps(part.at[k % 2], full.at[k], k % 2)
    for steps, others, block in (
        (scatters, waiting, n_block - 3),
        (gathers, [], n_block - 2),
    ):
        for s in range(rounds):
            slot = steps[s : s + 1] + others[s : s + 1]
            advance(slot)
            applied(block, s, rounds)
            advance(slot)
        extra(steps, others)
    applied(n_block - 1, 0, 1)
    for k in range(n_block):
        for s in range(n_grid - 1):
            drain(k, s)


def on_device(snapshots, jitter_code, slab_start, gamma, noise_var):
    n_row, n_col, n_grid = (lax.axis_size(a) for a in ("row", "col", "grid"))
    rows, snap = snapshots.shape
    group_rows = rows * n_grid
    points = gamma.shape[0]
    base = (lax.axis_index("row") * n_col + lax.axis_index("col")) * group_rows
    sensors = base + jnp.arange(group_rows, dtype=jnp.int32)
    pos = 64 * sensors + lax.dynamic_slice(jitter_code, (base,), (group_rows,)) + 32
    width = min(WIDTH, snap)
    n_block = snap // width
    dims = [n for n in (2, n_col // 2, n_row) if n > 1]
    landed, sums, length = [], [], points
    for n in dims:
        length //= n
        landed.append(pltpu.VMEM((2, n - 1, length, width), F32))
        sums.append(pltpu.VMEM((length, width), F32))
    n_peers = sum(n - 1 for n in dims)
    vmem = pl.BlockSpec(memory_space=pltpu.VMEM)
    steered, forms, norms = pl.pallas_call(
        functools.partial(kernel, (n_row, n_col, n_grid, GRID // points)),
        out_shape=(
            jax.ShapeDtypeStruct((group_rows, points), F32),
            jax.ShapeDtypeStruct((points, 128), F32),
            jax.ShapeDtypeStruct((points, 128), F32),
        ),
        in_specs=[
            pl.BlockSpec(memory_space=pltpu.SMEM),
            vmem,
            pl.BlockSpec(memory_space=pl.ANY),
        ],
        out_specs=(vmem, vmem, vmem),
        scratch_shapes=[
            pltpu.VMEM((n_block, n_grid, rows, width), BF16),
            pltpu.VMEM((n_grid, points, rows), BF16),
            pltpu.VMEM((n_grid, points, rows), BF16),
            pltpu.VMEM((2, points, width), F32),
            pltpu.VMEM((points, 128), F32),
            pltpu.VMEM((n_block, points, width), F32),
            pltpu.VMEM((points, width), BF16),
            pltpu.VMEM((points, width), BF16),
            *landed,
            *sums,
            pltpu.SemaphoreType.DMA((n_block,)),
            pltpu.SemaphoreType.DMA((2, n_block, n_grid - 1)),
            pltpu.SemaphoreType.DMA((2, n_block, n_grid - 1)),
            pltpu.SemaphoreType.DMA((4, n_peers)),
            pltpu.SemaphoreType.DMA((4, n_peers)),
        ],
        compiler_params=pltpu.CompilerParams(
            collective_id=0, has_side_effects=True, vmem_limit_bytes=56 << 20
        ),
    )(slab_start, pos.reshape(n_grid, 1, rows), snapshots)
    forms = forms[:, 0] / snap
    gamma_new = gamma * forms / (norms[:, 0] * (gamma + noise_var[0]))
    return (steered, gamma_new)


def solution(mesh):
    in_specs = (P(("row", "col", "grid"), None), P(), P("grid"), P("grid"), P())
    out_specs = (P(("row", "col"), "grid"), P("grid"))
    return jax.shard_map(
        on_device, mesh=mesh, in_specs=in_specs, out_specs=out_specs, check_vma=False
    )
```

```python
import functools

import jax
import jax.numpy as jnp
from jax import lax
from jax.experimental import pallas as pl
from jax.experimental.pallas import tpu as pltpu
from jax.sharding import PartitionSpec as P

GRID = 65536
WIDTH = 256
F32 = jnp.float32
BF16 = jnp.bfloat16
MESH = pl.DeviceIdType.MESH


def sine(turns):
    z = turns * turns
    p = F32(39.53581371)
    p = p * z + F32(-76.54965682)
    p = p * z + F32(81.60099819)
    p = p * z + F32(-41.34165493)
    p = p * z + F32(6.28318516)
    return p * turns


def split(x):
    hi = x.astype(BF16)
    return hi, (x - hi.astype(F32)).astype(BF16)


def kernel(
    sizes, start_ref, pos_ref, snaps_ref, out_ref, forms_ref, norms_ref, last_ref, proj_hi, proj_lo,
    held, steer_hi, steer_lo, part, part_norm, full, *rest,
):
    n_row, n_col, n_grid, stride = sizes
    dims = [d for d in ((2, "core"), (n_col // 2, "y"), (n_row, "row")) if d[0] > 1]
    landed, sums = rest[: len(dims)], rest[len(dims) : 2 * len(dims)]
    load_sem, z_send, z_recv, p_send, p_recv = rest[2 * len(dims) :]
    n_block, _, rows, width = held.shape
    points = part.shape[1]
    snap = n_block * width
    row, col, z = (lax.axis_index(a) for a in ("row", "col", "grid"))
    place = {"core": col % 2, "y": col // 2, "row": row}

    def peer(kind, n, p):
        other = lax.rem(place[kind] + p, n)
        if kind == "row":
            return (other, col, z)
        if kind == "core":
            return (row, (col // 2) * 2 + other, z)
        return (row, other * 2 + col % 2, z)

    peers = [peer(kind, n, p) for n, kind in dims for p in range(1, n)]
    up, down = (row, col, z + 1), (row, col, z - 1)
    loads = [
        pltpu.make_async_copy(
            snaps_ref.at[:, pl.ds(k * width, width)], held.at[k, z], load_sem.at[k]
        )
        for k in range(n_block)
    ]
    for load in loads:
        load.start()
    barrier = pltpu.get_barrier_semaphore()
    for device in peers:
        pl.semaphore_signal(barrier, inc=1, device_id=device, device_id_type=MESH)

    @pl.when(z + 1 < n_grid)
    def _():
        pl.semaphore_signal(barrier, inc=1, device_id=up, device_id_type=MESH)

    @pl.when(z > 0)
    def _():
        pl.semaphore_signal(barrier, inc=1, device_id=down, device_id_type=MESH)

    beside = jnp.minimum(z, 1) + jnp.minimum(n_grid - 1 - z, 1)
    pl.semaphore_wait(barrier, len(peers) + beside)

    def hop(k, s, direction, origin):
        return pltpu.make_async_remote_copy(
            src_ref=held.at[k, origin],
            dst_ref=held.at[k, origin],
            send_sem=z_send.at[direction, k, s],
            recv_sem=z_recv.at[direction, k, s],
            device_id=up if direction == 0 else down,
            device_id_type=MESH,
        )

    def can_send(s, direction):
        if direction == 0:
            return jnp.logical_and(z + 1 < n_grid, z - s >= 0), z - s
        return jnp.logical_and(z > 0, z + s < n_grid), z + s

    def can_receive(s, direction):
        if direction == 0:
            return z - s - 1 >= 0, z - s - 1
        return z + s + 1 < n_grid, z + s + 1

    def send(k, s):
        for direction in (0, 1):
            ok, origin = can_send(s, direction)

            @pl.when(ok)
            def _():
                hop(k, s, direction, origin).start()

    def receive(k, s):
        for direction in (0, 1):
            ok, origin = can_receive(s, direction)

            @pl.when(ok)
            def _():
                hop(k, s, direction, origin).wait_recv()

    def drain(k, s):
        for direction in (0, 1):
            ok, origin = can_send(s, direction)

            @pl.when(ok)
            def _():
                hop(k, s, direction, origin).wait_send()

    def reduce_steps(source, target, turn):
        lanes = pl.ds(0, source.shape[1])
        offsets, sems, at, count = [], [], 0, 0
        length = points
        for n, kind in dims:
            length //= n
            offsets.append((at, length))
            at = at + place[kind] * length
            sems.append(count)
            count += n - 1

        def aligned(index):
            return pl.multiple_of(index, 8)

        def scatter(a):
            n, kind = dims[a]
            size = offsets[a][1]
            cur = source if a == 0 else sums[a - 1].at[:, lanes]
            copies = []
            yield
            for p in range(1, n):
                other = lax.rem(place[kind] + p, n)
                copy = pltpu.make_async_remote_copy(
                    src_ref=cur.at[pl.ds(aligned(other * size), size), :],
                    dst_ref=landed[a].at[turn, p - 1, :, lanes],
                    send_sem=p_send.at[2 * turn, sems[a] + p - 1],
                    recv_sem=p_recv.at[2 * turn, sems[a] + p - 1],
                    device_id=peer(kind, n, p),
                    device_id_type=MESH,
                )
                copy.start()
                copies.append(copy)
            yield
            for copy in copies:
                copy.wait()
            total = cur[pl.ds(aligned(place[kind] * size), size), :]
            for p in range(1, n):
                total = total + landed[a][turn, p - 1, :, lanes]
            if a + 1 < len(dims):
                sums[a][:, lanes] = total
            else:
                target[pl.ds(aligned(at), size), :] = total
            yield

        def gather(a):
            n, kind = dims[a]
            base, size = offsets[a]
            mine = pl.ds(aligned(base + place[kind] * size), size)
            copies = []
            yield
            for p in range(1, n):
                copy = pltpu.make_async_remote_copy(
                    src_ref=target.at[mine, :],
                    dst_ref=target.at[mine, :],
                    send_sem=p_send.at[2 * turn + 1, sems[a] + p - 1],
                    recv_sem=p_recv.at[2 * turn + 1, sems[a] + p - 1],
                    device_id=peer(kind, n, p),
                    device_id_type=MESH,
                )
                copy.start()
                copies.append(copy)
            yield
            for copy in copies:
                copy.wait()
            yield

        scatters = [scatter(a) for a in range(len(dims))]
        gathers = [gather(a) for a in reversed(range(len(dims)))]
        for step in scatters + gathers:
            next(step)
        return scatters, gathers

    def steer():
        part_norm[...] = jnp.zeros_like(part_norm)
        tile = 16
        tiles = points // tile

        def body(i, carry):
            g, first = i // tiles, pl.multiple_of((i % tiles) * tile, tile)
            pos = pos_ref[g]
            point = start_ref[0] + stride * (
                first + lax.broadcasted_iota(jnp.int32, (tile, 1), 0)
            )
            phase = (point * pos - ((pos & 127) << 15)) << 10
            turns = phase.astype(F32) * F32(2.0**-32)
            value = sine(0.25 - jnp.abs(turns))
            hi, lo = split(value)
            steer_hi[g, pl.ds(first, tile), :] = hi
            steer_lo[g, pl.ds(first, tile), :] = lo
            square = jnp.sum(value * value, axis=1, keepdims=True)
            part_norm[pl.ds(first, tile), :] += jnp.broadcast_to(square, (tile, 128))
            return carry

        lax.fori_loop(0, n_grid * tiles, body, 0)

    def project(k, origin, fresh=False):
        block = held[k, origin]
        value = jnp.dot(steer_hi[origin], block, preferred_element_type=F32)
        value += jnp.dot(steer_lo[origin], block, preferred_element_type=F32)
        if fresh:
            part[k % 2] = value
        else:
            part[k % 2] += value

    def project_arrived(k, s):
        for direction in (0, 1):
            ok, origin = can_receive(s, direction)

            @pl.when(ok)
            def _():
                project(k, origin)

    def prepare(k):
        value = full[k]
        square = jnp.sum(value * value, axis=1, keepdims=True)
        square = jnp.broadcast_to(square, (points, 128))
        forms_ref[...] = square if k == 0 else forms_ref[...] + square
        hi, lo = split(value / snap)
        proj_hi[...] = hi
        proj_lo[...] = lo

    def apply(k, first, count):
        dims_nt = (((1,), (1,)), ((), ()))

        def body(g, carry):
            block = held[k, g]
            added = lax.dot_general(block, proj_hi[...], dims_nt, preferred_element_type=F32)
            added += lax.dot_general(block, proj_lo[...], dims_nt, preferred_element_type=F32)
            spot = pl.ds(pl.multiple_of(g * rows, rows), rows)
            out_ref[spot, :] = added if k == 0 else out_ref[spot, :] + added
            return carry

        lax.fori_loop(first, first + count, body, 0)

    def applied(k, s, rounds):
        if k < 0:
            return
        if s == 0:
            prepare(k)
        first, end = n_grid * s // rounds, n_grid * (s + 1) // rounds
        if end > first:
            apply(k, first, end - first)

    loads[0].wait()
    send(0, 0)
    if n_block > 1:
        loads[1].wait()
        send(1, 0)
    for load in loads[2:]:
        load.wait()
    steer()
    rounds = n_grid - 1
    def advance(steps):
        for step in steps:
            next(step)

    def extra(*lists):
        for steps in lists:
            for step in steps[rounds:]:
                next(step)
                next(step)

    scatters, gathers = reduce_steps(part_norm, norms_ref, 1)
    waiting = []
    for k in range(n_block):
        for s in range(rounds):
            slot = scatters[s : s + 1] + waiting[s : s + 1]
            advance(slot)
            if s == 0:
                project(k, z, fresh=True)
            receive(k, s)
            if s + 1 < rounds:
                send(k, s + 1)
            if s + 2 == rounds and k + 2 < n_block:
                send(k + 2, 0)
            project_arrived(k, s)
            applied(k - 3, s, rounds)
            advance(slot)
        extra(scatters, waiting)
        waiting = gathers
        scatters, gathers = reduce_steps(part.at[k % 2], full.at[k], k % 2)
    last_ref[...] = held[n_block - 1]
    for steps, others, block in (
        (scatters, waiting, n_block - 3),
        (gathers, [], n_block - 2),
    ):
        for s in range(rounds):
            slot = steps[s : s + 1] + others[s : s + 1]
            advance(slot)
            applied(block, s, rounds)
            advance(slot)
        extra(steps, others)
    prepare(n_block - 1)
    for k in range(n_block):
        for s in range(n_grid - 1):
            drain(k, s)


def finish(partly_ref, held_ref, hi_ref, lo_ref, out_ref):
    dims_nt = (((1,), (1,)), ((), ()))
    block = held_ref[0]
    added = lax.dot_general(block, hi_ref[...], dims_nt, preferred_element_type=F32)
    added += lax.dot_general(block, lo_ref[...], dims_nt, preferred_element_type=F32)
    out_ref[...] = partly_ref[...] + added


def on_device(snapshots, jitter_code, slab_start, gamma, noise_var):
    n_row, n_col, n_grid = (lax.axis_size(a) for a in ("row", "col", "grid"))
    rows, snap = snapshots.shape
    group_rows = rows * n_grid
    points = gamma.shape[0]
    base = (lax.axis_index("row") * n_col + lax.axis_index("col")) * group_rows
    sensors = base + jnp.arange(group_rows, dtype=jnp.int32)
    pos = 64 * sensors + lax.dynamic_slice(jitter_code, (base,), (group_rows,)) + 32
    width = min(WIDTH, snap)
    n_block = snap // width
    dims = [n for n in (2, n_col // 2, n_row) if n > 1]
    landed, sums, length = [], [], points
    for n in dims:
        length //= n
        landed.append(pltpu.VMEM((2, n - 1, length, width), F32))
        sums.append(pltpu.VMEM((length, width), F32))
    n_peers = sum(n - 1 for n in dims)
    vmem = pl.BlockSpec(memory_space=pltpu.VMEM)
    partly, forms, norms, held, proj_hi, proj_lo = pl.pallas_call(
        functools.partial(kernel, (n_row, n_col, n_grid, GRID // points)),
        out_shape=(
            jax.ShapeDtypeStruct((group_rows, points), F32),
            jax.ShapeDtypeStruct((points, 128), F32),
            jax.ShapeDtypeStruct((points, 128), F32),
            jax.ShapeDtypeStruct((n_grid, rows, width), BF16),
            jax.ShapeDtypeStruct((points, width), BF16),
            jax.ShapeDtypeStruct((points, width), BF16),
        ),
        in_specs=[
            pl.BlockSpec(memory_space=pltpu.SMEM),
            vmem,
            pl.BlockSpec(memory_space=pl.ANY),
        ],
        out_specs=(vmem,) * 6,
        scratch_shapes=[
            pltpu.VMEM((n_block, n_grid, rows, width), BF16),
            pltpu.VMEM((n_grid, points, rows), BF16),
            pltpu.VMEM((n_grid, points, rows), BF16),
            pltpu.VMEM((2, points, width), F32),
            pltpu.VMEM((points, 128), F32),
            pltpu.VMEM((n_block, points, width), F32),
            *landed,
            *sums,
            pltpu.SemaphoreType.DMA((n_block,)),
            pltpu.SemaphoreType.DMA((2, n_block, n_grid - 1)),
            pltpu.SemaphoreType.DMA((2, n_block, n_grid - 1)),
            pltpu.SemaphoreType.DMA((4, n_peers)),
            pltpu.SemaphoreType.DMA((4, n_peers)),
        ],
        compiler_params=pltpu.CompilerParams(
            collective_id=0, has_side_effects=True, vmem_limit_bytes=56 << 20
        ),
    )(slab_start, pos.reshape(n_grid, 1, rows), snapshots)
    whole = pl.BlockSpec((points, width), lambda i: (0, 0))
    tile = pl.BlockSpec((rows, points), lambda i: (i, 0))
    steered = pl.pallas_call(
        finish,
        grid=(n_grid,),
        out_shape=jax.ShapeDtypeStruct((group_rows, points), F32),
        in_specs=[tile, pl.BlockSpec((1, rows, width), lambda i: (i, 0, 0)), whole, whole],
        out_specs=tile,
    )(partly, held, proj_hi, proj_lo)
    forms = forms[:, 0] / snap
    gamma_new = gamma * forms / (norms[:, 0] * (gamma + noise_var[0]))
    return (steered, gamma_new)


def solution(mesh):
    in_specs = (P(("row", "col", "grid"), None), P(), P("grid"), P("grid"), P())
    out_specs = (P(("row", "col"), "grid"), P("grid"))
    return jax.shard_map(
        on_device, mesh=mesh, in_specs=in_specs, out_specs=out_specs, check_vma=False
    )
```

```python
import functools

import jax
import jax.numpy as jnp
from jax import lax
from jax.experimental import pallas as pl
from jax.experimental.pallas import tpu as pltpu
from jax.sharding import PartitionSpec as P

GRID = 65536
WIDTH = 256
F32 = jnp.float32
BF16 = jnp.bfloat16
MESH = pl.DeviceIdType.MESH


def sine(turns):
    z = turns * turns
    p = F32(39.53581371)
    p = p * z + F32(-76.54965682)
    p = p * z + F32(81.60099819)
    p = p * z + F32(-41.34165493)
    p = p * z + F32(6.28318516)
    return p * turns


def split(x):
    hi = x.astype(BF16)
    return hi, (x - hi.astype(F32)).astype(BF16)


def kernel(
    sizes, start_ref, pos_ref, snaps_ref, out_ref, forms_ref, norms_ref, last_ref, proj_hi, proj_lo,
    held, steer_hi, steer_lo, part, part_norm, full, *rest,
):
    n_row, n_col, n_grid, stride = sizes
    dims = [d for d in ((2, "core"), (n_col // 2, "y"), (n_row, "row")) if d[0] > 1]
    landed, sums = rest[: len(dims)], rest[len(dims) : 2 * len(dims)]
    load_sem, z_send, z_recv, p_send, p_recv = rest[2 * len(dims) :]
    n_block, _, rows, width = held.shape
    points = part.shape[1]
    snap = n_block * width
    row, col, z = (lax.axis_index(a) for a in ("row", "col", "grid"))
    place = {"core": col % 2, "y": col // 2, "row": row}

    def peer(kind, n, p):
        other = lax.rem(place[kind] + p, n)
        if kind == "row":
            return (other, col, z)
        if kind == "core":
            return (row, (col // 2) * 2 + other, z)
        return (row, other * 2 + col % 2, z)

    peers = [peer(kind, n, p) for n, kind in dims for p in range(1, n)]
    up, down = (row, col, z + 1), (row, col, z - 1)
    loads = [
        pltpu.make_async_copy(
            snaps_ref.at[:, pl.ds(k * width, width)], held.at[k, z], load_sem.at[k]
        )
        for k in range(n_block)
    ]
    for load in loads:
        load.start()
    barrier = pltpu.get_barrier_semaphore()
    for device in peers:
        pl.semaphore_signal(barrier, inc=1, device_id=device, device_id_type=MESH)

    @pl.when(z + 1 < n_grid)
    def _():
        pl.semaphore_signal(barrier, inc=1, device_id=up, device_id_type=MESH)

    @pl.when(z > 0)
    def _():
        pl.semaphore_signal(barrier, inc=1, device_id=down, device_id_type=MESH)

    beside = jnp.minimum(z, 1) + jnp.minimum(n_grid - 1 - z, 1)
    pl.semaphore_wait(barrier, len(peers) + beside)

    def hop(k, s, direction, origin):
        return pltpu.make_async_remote_copy(
            src_ref=held.at[k, origin],
            dst_ref=held.at[k, origin],
            send_sem=z_send.at[direction, k, s],
            recv_sem=z_recv.at[direction, k, s],
            device_id=up if direction == 0 else down,
            device_id_type=MESH,
        )

    def can_send(s, direction):
        if direction == 0:
            return jnp.logical_and(z + 1 < n_grid, z - s >= 0), z - s
        return jnp.logical_and(z > 0, z + s < n_grid), z + s

    def can_receive(s, direction):
        if direction == 0:
            return z - s - 1 >= 0, z - s - 1
        return z + s + 1 < n_grid, z + s + 1

    def send(k, s):
        for direction in (0, 1):
            ok, origin = can_send(s, direction)

            @pl.when(ok)
            def _():
                hop(k, s, direction, origin).start()

    def receive(k, s):
        for direction in (0, 1):
            ok, origin = can_receive(s, direction)

            @pl.when(ok)
            def _():
                hop(k, s, direction, origin).wait_recv()

    def drain(k, s):
        for direction in (0, 1):
            ok, origin = can_send(s, direction)

            @pl.when(ok)
            def _():
                hop(k, s, direction, origin).wait_send()

    def reduce_steps(source, target, turn):
        lanes = pl.ds(0, source.shape[1])
        offsets, sems, at, count = [], [], 0, 0
        length = points
        for n, kind in dims:
            length //= n
            offsets.append((at, length))
            at = at + place[kind] * length
            sems.append(count)
            count += n - 1

        def aligned(index):
            return pl.multiple_of(index, 8)

        def scatter(a):
            n, kind = dims[a]
            size = offsets[a][1]
            cur = source if a == 0 else sums[a - 1].at[:, lanes]
            copies = []
            yield
            for p in range(1, n):
                other = lax.rem(place[kind] + p, n)
                copy = pltpu.make_async_remote_copy(
                    src_ref=cur.at[pl.ds(aligned(other * size), size), :],
                    dst_ref=landed[a].at[turn, p - 1, :, lanes],
                    send_sem=p_send.at[2 * turn, sems[a] + p - 1],
                    recv_sem=p_recv.at[2 * turn, sems[a] + p - 1],
                    device_id=peer(kind, n, p),
                    device_id_type=MESH,
                )
                copy.start()
                copies.append(copy)
            yield
            for copy in copies:
                copy.wait()
            total = cur[pl.ds(aligned(place[kind] * size), size), :]
            for p in range(1, n):
                total = total + landed[a][turn, p - 1, :, lanes]
            if a + 1 < len(dims):
                sums[a][:, lanes] = total
            else:
                target[pl.ds(aligned(at), size), :] = total
            yield

        def gather(a):
            n, kind = dims[a]
            base, size = offsets[a]
            mine = pl.ds(aligned(base + place[kind] * size), size)
            copies = []
            yield
            for p in range(1, n):
                copy = pltpu.make_async_remote_copy(
                    src_ref=target.at[mine, :],
                    dst_ref=target.at[mine, :],
                    send_sem=p_send.at[2 * turn + 1, sems[a] + p - 1],
                    recv_sem=p_recv.at[2 * turn + 1, sems[a] + p - 1],
                    device_id=peer(kind, n, p),
                    device_id_type=MESH,
                )
                copy.start()
                copies.append(copy)
            yield
            for copy in copies:
                copy.wait()
            yield

        scatters = [scatter(a) for a in range(len(dims))]
        gathers = [gather(a) for a in reversed(range(len(dims)))]
        for step in scatters + gathers:
            next(step)
        return scatters, gathers

    def steer():
        part_norm[...] = jnp.zeros_like(part_norm)
        tile = 16
        tiles = points // tile

        def body(i, carry):
            g, first = i // tiles, pl.multiple_of((i % tiles) * tile, tile)
            pos = pos_ref[g]
            point = start_ref[0] + stride * (
                first + lax.broadcasted_iota(jnp.int32, (tile, 1), 0)
            )
            phase = (point * pos - ((pos & 127) << 15)) << 10
            turns = phase.astype(F32) * F32(2.0**-32)
            value = sine(0.25 - jnp.abs(turns))
            hi, lo = split(value)
            steer_hi[g, pl.ds(first, tile), :] = hi
            steer_lo[g, pl.ds(first, tile), :] = lo
            square = jnp.sum(value * value, axis=1, keepdims=True)
            part_norm[pl.ds(first, tile), :] += jnp.broadcast_to(square, (tile, 128))
            return carry

        lax.fori_loop(0, n_grid * tiles, body, 0)

    def project(k, origin, fresh=False):
        block = held[k, origin]
        value = jnp.dot(steer_hi[origin], block, preferred_element_type=F32)
        value += jnp.dot(steer_lo[origin], block, preferred_element_type=F32)
        if fresh:
            part[k % 2] = value
        else:
            part[k % 2] += value

    def project_arrived(k, s):
        for direction in (0, 1):
            ok, origin = can_receive(s, direction)

            @pl.when(ok)
            def _():
                project(k, origin)

    def prepare(k):
        value = full[k]
        square = jnp.sum(value * value, axis=1, keepdims=True)
        square = jnp.broadcast_to(square, (points, 128))
        forms_ref[...] = square if k == 0 else forms_ref[...] + square
        hi, lo = split(value / snap)
        proj_hi[...] = hi
        proj_lo[...] = lo

    def apply(k, first, count):
        dims_nt = (((1,), (1,)), ((), ()))

        def body(g, carry):
            block = held[k, g]
            added = lax.dot_general(block, proj_hi[...], dims_nt, preferred_element_type=F32)
            added += lax.dot_general(block, proj_lo[...], dims_nt, preferred_element_type=F32)
            spot = pl.ds(pl.multiple_of(g * rows, rows), rows)
            out_ref[spot, :] = added if k == 0 else out_ref[spot, :] + added
            return carry

        lax.fori_loop(first, first + count, body, 0)

    def applied(k, s, rounds):
        if k < 0:
            return
        if s == 0:
            prepare(k)
        first, end = n_grid * s // rounds, n_grid * (s + 1) // rounds
        if end > first:
            apply(k, first, end - first)

    loads[0].wait()
    send(0, 0)
    if n_block > 1:
        loads[1].wait()
        send(1, 0)
    for load in loads[2:]:
        load.wait()
    steer()
    rounds = n_grid - 1
    def advance(steps):
        for step in steps:
            next(step)

    def extra(*lists):
        for steps in lists:
            for step in steps[rounds:]:
                next(step)
                next(step)

    scatters, gathers = reduce_steps(part_norm, norms_ref, 1)
    waiting = []
    for k in range(n_block):
        for s in range(rounds):
            slot = scatters[s : s + 1] + waiting[s : s + 1]
            advance(slot)
            receive(k, s)
            if s + 1 < rounds:
                send(k, s + 1)
            if s + 2 == rounds and k + 2 < n_block:
                send(k + 2, 0)
            if s == 0:
                project(k, z, fresh=True)
            project_arrived(k, s)
            applied(k - 3, s, rounds)
            advance(slot)
        extra(scatters, waiting)
        waiting = gathers
        scatters, gathers = reduce_steps(part.at[k % 2], full.at[k], k % 2)
    last_ref[...] = held[n_block - 1]
    for steps, others, block in (
        (scatters, waiting, n_block - 3),
        (gathers, [], n_block - 2),
    ):
        for s in range(rounds):
            slot = steps[s : s + 1] + others[s : s + 1]
            advance(slot)
            applied(block, s, rounds)
            advance(slot)
        extra(steps, others)
    prepare(n_block - 1)
    for k in range(n_block):
        for s in range(n_grid - 1):
            drain(k, s)


def finish(partly_ref, held_ref, hi_ref, lo_ref, out_ref):
    dims_nt = (((1,), (1,)), ((), ()))
    block = held_ref[0]
    added = lax.dot_general(block, hi_ref[...], dims_nt, preferred_element_type=F32)
    added += lax.dot_general(block, lo_ref[...], dims_nt, preferred_element_type=F32)
    out_ref[...] = partly_ref[...] + added


def on_device(snapshots, jitter_code, slab_start, gamma, noise_var):
    n_row, n_col, n_grid = (lax.axis_size(a) for a in ("row", "col", "grid"))
    rows, snap = snapshots.shape
    group_rows = rows * n_grid
    points = gamma.shape[0]
    base = (lax.axis_index("row") * n_col + lax.axis_index("col")) * group_rows
    sensors = base + jnp.arange(group_rows, dtype=jnp.int32)
    pos = 64 * sensors + lax.dynamic_slice(jitter_code, (base,), (group_rows,)) + 32
    width = min(WIDTH, snap)
    n_block = snap // width
    dims = [n for n in (2, n_col // 2, n_row) if n > 1]
    landed, sums, length = [], [], points
    for n in dims:
        length //= n
        landed.append(pltpu.VMEM((2, n - 1, length, width), F32))
        sums.append(pltpu.VMEM((length, width), F32))
    n_peers = sum(n - 1 for n in dims)
    vmem = pl.BlockSpec(memory_space=pltpu.VMEM)
    partly, forms, norms, held, proj_hi, proj_lo = pl.pallas_call(
        functools.partial(kernel, (n_row, n_col, n_grid, GRID // points)),
        out_shape=(
            jax.ShapeDtypeStruct((group_rows, points), F32),
            jax.ShapeDtypeStruct((points, 128), F32),
            jax.ShapeDtypeStruct((points, 128), F32),
            jax.ShapeDtypeStruct((n_grid, rows, width), BF16),
            jax.ShapeDtypeStruct((points, width), BF16),
            jax.ShapeDtypeStruct((points, width), BF16),
        ),
        in_specs=[
            pl.BlockSpec(memory_space=pltpu.SMEM),
            vmem,
            pl.BlockSpec(memory_space=pl.ANY),
        ],
        out_specs=(vmem,) * 6,
        scratch_shapes=[
            pltpu.VMEM((n_block, n_grid, rows, width), BF16),
            pltpu.VMEM((n_grid, points, rows), BF16),
            pltpu.VMEM((n_grid, points, rows), BF16),
            pltpu.VMEM((2, points, width), F32),
            pltpu.VMEM((points, 128), F32),
            pltpu.VMEM((n_block, points, width), F32),
            *landed,
            *sums,
            pltpu.SemaphoreType.DMA((n_block,)),
            pltpu.SemaphoreType.DMA((2, n_block, n_grid - 1)),
            pltpu.SemaphoreType.DMA((2, n_block, n_grid - 1)),
            pltpu.SemaphoreType.DMA((4, n_peers)),
            pltpu.SemaphoreType.DMA((4, n_peers)),
        ],
        compiler_params=pltpu.CompilerParams(
            collective_id=0, has_side_effects=True, vmem_limit_bytes=56 << 20
        ),
    )(slab_start, pos.reshape(n_grid, 1, rows), snapshots)
    whole = pl.BlockSpec((points, width), lambda i: (0, 0))
    tile = pl.BlockSpec((rows, points), lambda i: (i, 0))
    steered = pl.pallas_call(
        finish,
        grid=(n_grid,),
        out_shape=jax.ShapeDtypeStruct((group_rows, points), F32),
        in_specs=[tile, pl.BlockSpec((1, rows, width), lambda i: (i, 0, 0)), whole, whole],
        out_specs=tile,
    )(partly, held, proj_hi, proj_lo)
    forms = forms[:, 0] / snap
    gamma_new = gamma * forms / (norms[:, 0] * (gamma + noise_var[0]))
    return (steered, gamma_new)


def solution(mesh):
    in_specs = (P(("row", "col", "grid"), None), P(), P("grid"), P("grid"), P())
    out_specs = (P(("row", "col"), "grid"), P("grid"))
    return jax.shard_map(
        on_device, mesh=mesh, in_specs=in_specs, out_specs=out_specs, check_vma=False
    )
```
